32 devices in a mesh: col: 2 (over x), row: 16 (over z, y, core).
Axes of the slice: x: 2, y: 2, z: 4, core: 2. Of those that a mesh axis runs over, the one named last changes fastest.
Arguments:
- residual: bfloat16 [1024, 2880], P('row'), may hold values from -6 to 6
- query_states: bfloat16 [1024, 4096], P('row', 'col'), may hold values from -48 to 48
- key_states: bfloat16 [1024, 512], P('row'), may hold values from -24 to 24
- value_states: bfloat16 [1024, 512], P('row'), may hold values from -6 to 6
- segment_ids: int32 [1024], P('row'), may hold values from 0 to 3, never falling along the last dimension, each value on 1 to 512 neighbouring positions
- sink_logits: float32 [64], P('col'), may hold values from -2 to 4
- w_out: bfloat16 [4096, 2880], P('col'), may hold values from -0.375 to 0.375
- norm_gain: float32 [2880], replicated, may hold values from 0.5 to 1.5
- expert_ids: int32 [1024, 4], P('row'), may hold values from 0 to 15, all different within a row; in each aligned block of 64 rows (0 to 63, 64 to 127, ...) at most 32 rows name the same one
- route_weight: float32 [1024, 4], P('row'), may hold values from 0.05 to 0.45
- w_gate_up: bfloat16 [16, 2, 2880, 2880], P('row', None, None, 'col'), may hold values from -0.109375 to 0.109375
- w_down: bfloat16 [16, 2880, 2880], P('row', 'col'), may hold values from -0.109375 to 0.109375
Outputs:
- layer_out: bfloat16 [1024, 2880], P('row', 'col')
The draws below stay inside these ranges and needn't reach their ends.
Inputs may be any that keep to these rules, and one draw needn't show every extreme that they name: `expert_ids`: each token names 4 different experts; among the 64 tokens of one index of row no expert is named by more than 32 tokens, and in every draw some expert is named by exactly 32 of them. `segment_ids`: segment numbers never fall along the tokens.
All inputs are finite; a program needn't handle non-finite values.
Results may differ from the reference program's by a relative error of at most 0.018.
Values may be sent and summed in bfloat16 or wider, within the bound.
A program may use at most 128 MiB of HBM per device.

```python
import math
import jax
import jax.numpy as jnp
import numpy as np
from jax import lax

D = 2880
HEADS = 64
KV_HEADS = 8
HEAD_DIM = 64
WINDOW = 128
FF = 2880
TOP = 4
TOK_ROW = 64
TOKENS = 1024
EXPERTS = 16
CAP = 32
N_ROW = 16


def shared_keys(key):
    base = jax.random.truncated_normal(jax.random.fold_in(key, 11), -6.0, 6.0, (TOKENS, KV_HEADS, HEAD_DIM), jnp.float32)
    return base


def draw_key_states(key, part):
    base = shared_keys(key)
    chosen = base
    return chosen.reshape(TOKENS, KV_HEADS * HEAD_DIM).astype(jnp.bfloat16)


def draw_query_states(key, part):
    drawn = jax.random.truncated_normal(jax.random.fold_in(key, 23), -6.0, 6.0, (TOKENS, HEADS * HEAD_DIM), jnp.float32)
    return drawn.astype(jnp.bfloat16)


def block_levels(key, dims, split, smallest, top_value):
    level = 1.0
    for axis_at, blocks in split:
        steps = jax.random.uniform(jax.random.fold_in(jax.random.fold_in(key, 6), axis_at), (blocks,), jnp.float32, smallest / len(split), top_value / len(split))
        level = level * jnp.repeat(jnp.exp(steps), dims[axis_at] // blocks).reshape((-1,) + (1,) * (len(dims) - 1 - axis_at))
    return level


def length_profile(count, total, reach, skew):
    portions = [(1 << 20) // math.isqrt(standing ** skew) + 1 for standing in range(2, count + 1)]
    spare, counts = total - reach - (count - 1), [1] * (count - 1)
    while spare > 0:
        candidates = [i for i in range(count - 1) if counts[i] < reach]
        whole, left = sum([portions[i] for i in candidates]), spare
        for i in candidates:
            addition = min(reach - counts[i], max(1, left * portions[i] // whole), spare)
            counts[i] = counts[i] + addition
            spare = spare - addition
    return np.array([reach] + counts)


def uneven_parts(own_key, amount, total, limit, skew):
    if amount == 2:
        one = jax.random.randint(own_key, (), max(1, total - limit), min(limit, total - 1) + 1)
        return jnp.stack([one, total - one])
    lengths = jnp.asarray(length_profile(amount, total, limit, skew), jnp.int32)
    pairs = (amount - 1) // 2
    donor, sink = lengths[1:1 + 2 * pairs:2], lengths[2:2 + 2 * pairs:2]
    room = jnp.minimum(donor - 1, limit - sink)
    moved = jax.random.randint(jax.random.fold_in(own_key, 1), (pairs,), 0, 1 << 20) % (room + 1)
    lengths = lengths.at[1:1 + 2 * pairs:2].set(donor - moved).at[2:2 + 2 * pairs:2].set(sink + moved)
    return lengths[jax.random.permutation(jax.random.fold_in(own_key, 2), amount)]


def assign_block(stream_key, own, number, rows, number_of, top, reach, lean):
    order = jax.random.permutation(stream_key, number_of)
    heavy_load, common = shares(number_of, rows * top, reach, lean, True), shares(number_of, rows * top, reach, lean, False)
    places = jnp.arange(number_of)

    def named(sizes, rotation):
        used = int((sizes > 0).sum())
        fixed = max(1, used // 4)
        moved = fixed + (places - fixed + rotation * (used - fixed)) % max(1, number_of - fixed)
        return jnp.zeros((number_of,), jnp.int32).at[order[jnp.where(places < fixed, places, moved)]].set(jnp.asarray(sizes, jnp.int32))

    sizes = jnp.where(number % 4 == 0, named(heavy_load, number // 4), named(common, number - number // 4 - 1))
    mixed = jax.random.permutation(jax.random.fold_in(own, 3), number_of)
    source_of, sink = mixed[0:number_of // 2 * 2:2], mixed[1:number_of // 2 * 2:2]
    margin = jnp.minimum(sizes[source_of] - 1, reach - sizes[sink]) // 2
    margin = jnp.where((source_of == order[0]) | (sink == order[0]) | (sizes[sink] == 0), 0, jnp.maximum(margin, 0))
    moved = jax.random.randint(jax.random.fold_in(own, 4), (number_of // 2,), 0, 1 << 20) % (margin + 1)
    sizes = sizes.at[source_of].add(-moved).at[sink].add(moved)
    labels = jnp.searchsorted(jnp.cumsum(sizes), jnp.arange(rows * top), side="right").astype(jnp.int32)
    listing = labels.reshape(top, rows).T
    listing = listing[jax.random.permutation(jax.random.fold_in(own, 1), rows)]
    rotation = jax.random.randint(jax.random.fold_in(own, 2), (rows, 1), 0, top)
    return jnp.take_along_axis(listing, (jnp.arange(top)[None, :] + rotation) % top, axis=1)


def shares(amount, total, limit, lean, full):
    weights = [(1 << 20) // math.isqrt(rank ** lean) + 1 for rank in range(1, amount + 1)]
    largest = limit if full else min(limit, max(-(-total // amount), total * weights[0] // sum(weights)))
    least = 1 if total - largest >= amount - 1 else 0
    given, spare = [largest] + [least] * (amount - 1), total - largest - least * (amount - 1)
    while spare > 0:
        candidates = [i for i in range(1, amount) if given[i] < largest] or [i for i in range(1, amount) if given[i] < limit]
        pool, left = sum([weights[i] for i in candidates]), spare
        for i in candidates:
            more = min(limit - given[i], max(1, left * weights[i] // pool), spare)
            given[i] = given[i] + more
            spare = spare - more
    return np.array(given)


def noise(rng, extent, deviation, most, split=(), kind=jnp.bfloat16):
    result = deviation * jax.random.normal(rng, extent, jnp.float32)
    if split:
        result = result * block_levels(rng, extent, split, -0.22, 0.18)
    return jnp.clip(result, -most, most).astype(kind)


def setup_inputs(seed: int = 0) -> dict:
    keys = jax.random.split(jax.random.key(seed), 13)
    residual = noise(keys[0], (TOKENS, D), 1.0, 6.0, ((0, 16),))
    query_states = draw_query_states(jax.random.fold_in(keys[12], 71), 0)
    key_states = draw_key_states(jax.random.fold_in(keys[12], 71), 0)
    value_states = noise(keys[3], (TOKENS, KV_HEADS * HEAD_DIM), 1.0, 6.0, ((0, 16),))
    segment_ids = jnp.searchsorted(jnp.cumsum(uneven_parts(keys[4], max(2, TOKENS // (2 * WINDOW)), TOKENS, min(4 * WINDOW, TOKENS // 2), 2)), jnp.arange(TOKENS), side="right").astype(jnp.int32)
    sink_logits = jnp.clip(-2.0 + 6.0 * jax.random.uniform(keys[5], (HEADS,), jnp.float32) ** block_levels(keys[5], (HEADS,), ((0, 2),), -0.2, 0.2), -2.0, 4.0)
    w_out = noise(keys[6], (HEADS * HEAD_DIM, D), (HEADS * HEAD_DIM // 16) ** -0.5, 0.375, ((0, 2),))
    norm_gain = jnp.clip(1.0 + 0.1 * jax.random.normal(keys[7], (D,), jnp.float32), 0.5, 1.5)
    expert_ids_keys = jax.random.split(jax.random.fold_in(keys[8], 1), TOKENS // TOK_ROW)
    expert_ids_turns = jax.random.permutation(jax.random.fold_in(keys[8], 3), TOKENS // TOK_ROW)
    expert_ids = jax.vmap(lambda own, number: assign_block(jax.random.fold_in(keys[8], 2), own, number, TOK_ROW, EXPERTS, TOP, CAP, 2))(expert_ids_keys, expert_ids_turns).reshape((TOKENS, TOP))
    route_weight = jnp.clip(0.05 + 0.39999999 * jax.random.uniform(keys[9], (TOKENS, TOP), jnp.float32) ** block_levels(keys[9], (TOKENS, TOP), ((0, 16),), -0.2, 0.2), 0.05, 0.45)
    w_gate_up = noise(keys[10], (EXPERTS, 2, D, FF), D ** -0.5, 0.109375, ((0, 16), (3, 2)))
    w_down = noise(keys[11], (EXPERTS, FF, D), FF ** -0.5, 0.109375, ((0, 16), (1, 2)))
    return dict(residual=residual, query_states=query_states, key_states=key_states, value_states=value_states, segment_ids=segment_ids, sink_logits=sink_logits, w_out=w_out, norm_gain=norm_gain, expert_ids=expert_ids, route_weight=route_weight, w_gate_up=w_gate_up, w_down=w_down)


epsilon = 1e-05
masked_score = -1e+30

def normalize(stream_rows, norm_gain):
    values32 = stream_rows.astype(jnp.float32)
    square_mean = lax.optimization_barrier(jnp.mean(values32 * values32, axis=-1, keepdims=True))
    return (values32 * lax.rsqrt(square_mean + epsilon) * norm_gain).astype(jnp.bfloat16)

def reference(residual, query_states, key_states, value_states, segment_ids, sink_logits, w_out, norm_gain, expert_ids, route_weight, w_gate_up, w_down):
    group_size = HEADS // KV_HEADS
    queries_all = query_states.astype(jnp.float32).reshape(TOKENS, KV_HEADS, group_size, HEAD_DIM)
    padding = jnp.zeros((WINDOW, KV_HEADS * HEAD_DIM), jnp.float32)
    keys_padded = jnp.concatenate([padding, key_states.astype(jnp.float32)], 0).reshape(TOKENS + WINDOW, KV_HEADS, HEAD_DIM)
    values_padded = jnp.concatenate([padding, value_states.astype(jnp.float32)], 0).reshape(TOKENS + WINDOW, KV_HEADS, HEAD_DIM)
    segments_padded = jnp.concatenate([jnp.full((WINDOW,), -1, jnp.int32), segment_ids], 0)
    sink_groups = sink_logits.reshape(KV_HEADS, group_size, 1, 1)

    def attend_block(block_at):
        start = block_at * WINDOW
        query_block = lax.dynamic_slice_in_dim(queries_all, start, WINDOW, 0)
        key_block = lax.dynamic_slice_in_dim(keys_padded, start, 2 * WINDOW, 0)
        value_block = lax.dynamic_slice_in_dim(values_padded, start, 2 * WINDOW, 0)
        key_segments = lax.dynamic_slice_in_dim(segments_padded, start, 2 * WINDOW, 0)
        query_segments = lax.dynamic_slice_in_dim(segment_ids, start, WINDOW, 0)
        query_position = start + jnp.arange(WINDOW, dtype=jnp.int32)
        key_position = start - WINDOW + jnp.arange(2 * WINDOW, dtype=jnp.int32)
        allowed = (key_position[None, :] >= 0) & (key_position[None, :] <= query_position[:, None])
        allowed = allowed & (key_position[None, :] > query_position[:, None] - WINDOW)
        allowed = allowed & (key_segments[None, :] == query_segments[:, None])
        scores = jnp.einsum('tgjd,lgd->gjtl', query_block, key_block) * HEAD_DIM ** (-0.5)
        scores = jnp.where(allowed[None, None], scores, masked_score)
        peak_score = jnp.maximum(lax.optimization_barrier(jnp.max(scores, axis=-1, keepdims=True)), sink_groups)
        numerator = jnp.exp(scores - peak_score)
        denominator = jnp.exp(sink_groups - peak_score) + lax.optimization_barrier(jnp.sum(numerator, axis=-1, keepdims=True))
        weights = (numerator / denominator).astype(jnp.bfloat16)
        weights = lax.optimization_barrier(weights).astype(jnp.float32)
        attended_block = jnp.einsum('gjtl,lgd->tgjd', weights, value_block)
        return attended_block.astype(jnp.bfloat16).reshape(WINDOW, HEADS * HEAD_DIM)
    attended = lax.map(attend_block, jnp.arange(TOKENS // WINDOW, dtype=jnp.int32)).reshape(TOKENS, HEADS * HEAD_DIM)
    stream = (residual.astype(jnp.float32) + jnp.dot(attended, w_out, preferred_element_type=jnp.float32)).astype(jnp.bfloat16)
    normed = normalize(stream, norm_gain)
    block_ids = expert_ids.reshape(N_ROW, TOK_ROW * TOP)
    expert_hot = (block_ids[:, :, None] == jnp.arange(EXPERTS, dtype=jnp.int32)[None, None, :]).astype(jnp.int32)
    earlier = jnp.cumsum(expert_hot, axis=1) - expert_hot
    slot_of = lax.optimization_barrier(jnp.sum(earlier * expert_hot, axis=2))
    block_index = jnp.arange(N_ROW, dtype=jnp.int32)[:, None]
    place = (block_ids * (N_ROW * CAP) + block_index * CAP + slot_of).reshape(-1).astype(jnp.int32)
    owner = jnp.repeat(jnp.arange(TOKENS, dtype=jnp.int32), TOP)
    table = jnp.full((EXPERTS * N_ROW * CAP,), -1, jnp.int32).at[place].set(owner).reshape(EXPERTS, N_ROW * CAP)

    def one_expert(expert_at):
        index_row = table[expert_at]
        picked = jnp.take(normed, jnp.maximum(index_row, 0), axis=0)
        slot_rows = jnp.where((index_row >= 0)[:, None], picked, jnp.zeros_like(picked))
        gate_part = jnp.dot(slot_rows, w_gate_up[expert_at, 0], preferred_element_type=jnp.float32)
        up_part = jnp.dot(slot_rows, w_gate_up[expert_at, 1], preferred_element_type=jnp.float32)
        active = ((up_part + 1.0) * gate_part * jax.nn.sigmoid(1.702 * gate_part)).astype(jnp.bfloat16)
        return jnp.dot(active, w_down[expert_at], preferred_element_type=jnp.float32).astype(jnp.bfloat16)
    expert_outputs = lax.map(one_expert, jnp.arange(EXPERTS, dtype=jnp.int32)).reshape(EXPERTS * N_ROW * CAP, D)
    gathered = jnp.take(expert_outputs, place.reshape(TOKENS, TOP), axis=0).astype(jnp.float32)
    expert_mix = lax.optimization_barrier(jnp.sum(route_weight[:, :, None] * gathered, axis=1))
    return (stream.astype(jnp.float32) + expert_mix).astype(jnp.bfloat16)
```

```python
import jax
import jax.numpy as jnp
from jax import lax
from jax.sharding import PartitionSpec as P

HEADS = 64
KV_HEADS = 8
HEAD_DIM = 64
WINDOW = 128
TOP = 4


epsilon = 1e-05
masked_score = -1e30


def shifted(shard, axis, by):
    size = lax.axis_size(axis)
    pairs = [(i, i + by) for i in range(size) if 0 <= i + by < size]
    return lax.ppermute(shard, axis, pairs)


def normalize(stream_rows, norm_gain):
    values32 = stream_rows.astype(jnp.float32)
    square_mean = jnp.mean(values32 * values32, axis=-1, keepdims=True)
    return (values32 * lax.rsqrt(square_mean + epsilon) * norm_gain).astype(jnp.bfloat16)


def attend(query_groups, key_groups, value_groups, allowed, sink_groups):
    scores = jnp.einsum(
        "tgjd,lgd->gjtl", query_groups, key_groups, preferred_element_type=jnp.float32
    )
    scores = scores * query_groups.shape[-1] ** (-0.5)
    scores = jnp.where(allowed[None, None], scores, masked_score)
    peak_score = jnp.maximum(jnp.max(scores, axis=-1, keepdims=True), sink_groups)
    numerator = jnp.exp(scores - peak_score)
    denominator = jnp.exp(sink_groups - peak_score) + jnp.sum(numerator, axis=-1, keepdims=True)
    weights = (numerator / denominator).astype(jnp.bfloat16)
    return jnp.einsum(
        "gjtl,lgd->tgjd", weights, value_groups, preferred_element_type=jnp.float32
    ).astype(jnp.bfloat16)


def local(
    residual,
    query_states,
    key_states,
    value_states,
    segment_ids,
    sink_logits,
    w_out,
    norm_gain,
    expert_ids,
    route_weight,
    w_gate_up,
    w_down,
):
    tok_rows = query_states.shape[0]
    row_count = lax.axis_size("row")
    col_count = lax.axis_size("col")
    row_index = lax.axis_index("row")
    col_index = lax.axis_index("col")
    local_heads = sink_logits.shape[0]
    group_size = HEADS // KV_HEADS
    if local_heads >= group_size:
        kv_count = local_heads // group_size
        kv_first = col_index * kv_count
    else:
        kv_count = 1
        kv_first = col_index * local_heads // group_size
    kv_width = kv_count * HEAD_DIM
    own_keys = lax.dynamic_slice_in_dim(key_states, kv_first * HEAD_DIM, kv_width, 1)
    own_values = lax.dynamic_slice_in_dim(value_states, kv_first * HEAD_DIM, kv_width, 1)
    shift_count = (WINDOW + tok_rows - 2) // tok_rows
    key_parts = []
    value_parts = []
    segment_parts = []
    start_parts = []
    for offset in range(shift_count, 0, -1):
        arrived = shifted((own_keys, own_values, segment_ids), "row", offset)
        key_parts.append(arrived[0])
        value_parts.append(arrived[1])
        segment_parts.append(arrived[2])
        start_parts.append((row_index - offset) * tok_rows)
    key_parts.append(own_keys)
    value_parts.append(own_values)
    segment_parts.append(segment_ids)
    start_parts.append(row_index * tok_rows)
    key_groups = jnp.concatenate(key_parts, 0).reshape(-1, kv_count, HEAD_DIM)
    value_groups = jnp.concatenate(value_parts, 0).reshape(-1, kv_count, HEAD_DIM)
    key_segments = jnp.concatenate(segment_parts, 0)
    positions = jnp.arange(tok_rows, dtype=jnp.int32)
    key_position = jnp.concatenate([start + positions for start in start_parts], 0)
    query_position = row_index * tok_rows + positions
    allowed = (key_position[None, :] >= 0) & (key_position[None, :] <= query_position[:, None])
    allowed = allowed & (key_position[None, :] > query_position[:, None] - WINDOW)
    allowed = allowed & (key_segments[None, :] == segment_ids[:, None])
    query_groups = query_states.reshape(tok_rows, kv_count, local_heads // kv_count, HEAD_DIM)
    sink_groups = sink_logits.reshape(kv_count, local_heads // kv_count, 1, 1)
    attended = attend(query_groups, key_groups, value_groups, allowed, sink_groups).reshape(
        tok_rows, local_heads * HEAD_DIM
    )
    partial_value = jnp.dot(attended, w_out, preferred_element_type=jnp.float32)
    feature_count = residual.shape[1] // col_count
    experts_all = w_gate_up.shape[0] * row_count
    slot_cap = max(2, 2 * TOP * tok_rows // experts_all)
    routing = jnp.concatenate([expert_ids.astype(jnp.float32), route_weight], 1)
    routing = lax.all_gather(routing, "row", axis=0, tiled=False)
    names_mine = routing[:, :, :TOP] == row_index.astype(jnp.float32)
    mine = jnp.any(names_mine, axis=2)
    weight = jnp.sum(jnp.where(names_mine, routing[:, :, TOP:], 0.0), axis=2)
    slot_of = jnp.cumsum(mine.astype(jnp.int32), axis=1) - 1
    slots = jnp.arange(slot_cap, dtype=jnp.int32)
    chosen = mine[:, None, :] & (slot_of[:, None, :] == slots[None, :, None])
    selector = chosen.astype(jnp.bfloat16)
    combine = jnp.where(chosen, weight[:, None, :], 0.0)
    expert_gate_up = w_gate_up[0]
    expert_down = w_down[0]
    summed = lax.psum(partial_value.astype(jnp.bfloat16), "col").astype(jnp.float32)
    stream = (residual.astype(jnp.float32) + summed).astype(jnp.bfloat16)
    stream_part = lax.dynamic_slice_in_dim(stream, col_index * feature_count, feature_count, 1)
    source_rows = normalize(stream, norm_gain)
    gathered = lax.all_gather(source_rows, "row", axis=0, tiled=False)
    packed = jnp.einsum(
        "nst,ntd->nsd", selector, gathered, preferred_element_type=jnp.float32
    ).astype(jnp.bfloat16).reshape(row_count * slot_cap, -1)
    gate = jnp.dot(packed, expert_gate_up[0], preferred_element_type=jnp.float32)
    up = jnp.dot(packed, expert_gate_up[1], preferred_element_type=jnp.float32)
    active = ((up + 1.0) * gate * jax.nn.sigmoid(1.702 * gate)).astype(jnp.bfloat16)
    expert_partial = jnp.dot(active, expert_down, preferred_element_type=jnp.float32)
    scaled = expert_partial.reshape(row_count, slot_cap, -1) * jnp.sum(combine, 2)[:, :, None]
    mixed = jnp.einsum(
        "nst,nsd->ntd", selector, scaled.astype(jnp.bfloat16), preferred_element_type=jnp.float32
    ).astype(jnp.bfloat16).reshape(row_count * tok_rows, -1)
    mixed = lax.psum_scatter(mixed, "row", scatter_dimension=0, tiled=True)
    mixed = lax.psum_scatter(mixed, "col", scatter_dimension=1, tiled=True)
    return (stream_part.astype(jnp.float32) + mixed.astype(jnp.float32)).astype(jnp.bfloat16)


def solution(mesh):
    in_specs = (
        P("row", None),
        P("row", "col"),
        P("row", None),
        P("row", None),
        P("row"),
        P("col"),
        P("col", None),
        P(),
        P("row", None),
        P("row", None),
        P("row", None, None, "col"),
        P("row", "col", None),
    )
    out_specs = P("row", "col")
    return jax.shard_map(local, mesh=mesh, in_specs=in_specs, out_specs=out_specs, check_vma=False)
```

```python
import jax
import jax.numpy as jnp
from jax import lax
from jax.experimental import pallas as pl
from jax.experimental.pallas import tpu as pltpu
from jax.sharding import PartitionSpec as P

HEADS = 64
KV_HEADS = 8
HEAD_DIM = 64
WINDOW = 128
TOP = 4


epsilon = 1e-05
masked_score = -1e30


def shifted(shard, axis, by):
    size = lax.axis_size(axis)
    pairs = [(i, i + by) for i in range(size) if 0 <= i + by < size]
    return lax.ppermute(shard, axis, pairs)


def normalize(stream_rows, norm_gain):
    values32 = stream_rows.astype(jnp.float32)
    square_mean = jnp.mean(values32 * values32, axis=-1, keepdims=True)
    return (values32 * lax.rsqrt(square_mean + epsilon) * norm_gain).astype(jnp.bfloat16)


def attend(query_groups, key_groups, value_groups, allowed, sink_groups):
    scores = jnp.einsum(
        "tgjd,lgd->gjtl", query_groups, key_groups, preferred_element_type=jnp.float32
    )
    scores = scores * query_groups.shape[-1] ** (-0.5)
    scores = jnp.where(allowed[None, None], scores, masked_score)
    peak_score = jnp.maximum(jnp.max(scores, axis=-1, keepdims=True), sink_groups)
    numerator = jnp.exp(scores - peak_score)
    denominator = jnp.exp(sink_groups - peak_score) + jnp.sum(numerator, axis=-1, keepdims=True)
    weights = (numerator / denominator).astype(jnp.bfloat16)
    return jnp.einsum(
        "gjtl,lgd->tgjd", weights, value_groups, preferred_element_type=jnp.float32
    ).astype(jnp.bfloat16)


MESH = pl.DeviceIdType.MESH
VMEM = pl.BlockSpec(memory_space=pltpu.VMEM)
HALVES = 2
VMEM_BYTES = 60 * 1024 * 1024


def ring_place(row, chips):
    chip = lax.div(row, 2)
    along = lax.div(chip, 2)
    return jnp.where(lax.rem(chip, 2) == 0, along, chips - 1 - along)


def ring_row(place, chips, core):
    place = lax.rem(place + chips, chips)
    chip = jnp.where(place < chips // 2, 2 * place, 2 * (chips - 1 - place) + 1)
    return 2 * chip + core


def greet(devices):
    barrier = pltpu.get_barrier_semaphore()
    for device in devices:
        pl.semaphore_signal(barrier, inc=1, device_id=device, device_id_type=MESH)
    pl.semaphore_wait(barrier, len(devices))


def remote(src, dst, send, recv, device):
    return pltpu.make_async_remote_copy(
        src_ref=src, dst_ref=dst, send_sem=send, recv_sem=recv, device_id=device,
        device_id_type=MESH,
    )


def halo_kernel(rows, shifts, kv_ref, meta_ref, kv_out, meta_out, kv_send, kv_recv, m_send, m_recv, l_sem):
    row = lax.axis_index("row")
    others = [{"row": lax.rem(row + step, rows)} for step in range(1, rows)]
    greet(others)
    copies = []
    for shift in range(1, shifts + 1):
        copies.append(
            remote(kv_ref, kv_out.at[shift - 1], kv_send.at[shift - 1], kv_recv.at[shift - 1],
                   others[shift - 1])
        )
    for step in range(1, rows):
        copies.append(
            remote(meta_ref, meta_out.at[row], m_send.at[step - 1], m_recv.at[step - 1],
                   others[step - 1])
        )
    for copy in copies:
        copy.start()
    mine = pltpu.make_async_copy(meta_ref, meta_out.at[row], l_sem)
    mine.start()
    for shift in range(1, shifts + 1):
        copies[shift - 1].wait()
    for step in range(1, rows):
        copies[shifts + step - 1].wait_send()
        source = lax.rem(row - step + rows, rows)
        remote(meta_ref, meta_out.at[source], m_send.at[step - 1], m_recv.at[step - 1],
               others[step - 1]).wait_recv()
    mine.wait()


def halo(kv, meta, rows, shifts):
    return pl.pallas_call(
        lambda *refs: halo_kernel(rows, shifts, *refs),
        out_shape=(
            jax.ShapeDtypeStruct((shifts, *kv.shape), kv.dtype),
            jax.ShapeDtypeStruct((rows, *meta.shape), meta.dtype),
        ),
        in_specs=[VMEM] * 2,
        out_specs=(VMEM, VMEM),
        scratch_shapes=[
            pltpu.SemaphoreType.DMA((shifts,)),
            pltpu.SemaphoreType.DMA((shifts,)),
            pltpu.SemaphoreType.DMA((rows,)),
            pltpu.SemaphoreType.DMA((rows,)),
            pltpu.SemaphoreType.DMA,
        ],
        compiler_params=pltpu.CompilerParams(
            collective_id=1, has_side_effects=True, vmem_limit_bytes=16 * 1024 * 1024
        ),
        name="halo",
    )(kv, meta)


def ring_halves(distance, half_way, way):
    return range(HALVES) if distance < half_way else [way]


def spread_kernel(rows, partial_ref, residual_ref, gain_ref, stream_ref, out_ref, part_in,
                  x_sem, send, recv, sib_send, sib_recv):
    chips = rows // 2
    half_way = chips // 2
    row = lax.axis_index("row")
    col = lax.axis_index("col")
    core = lax.rem(row, 2)
    place = ring_place(row, chips)
    sibling = {"row": row + 1 - 2 * core}
    partner = {"col": 1 - col}
    ways = [{"row": ring_row(place + 1, chips, core)}, {"row": ring_row(place - 1, chips, core)}]
    greet([sibling, partner] + ways)
    cross = remote(partial_ref, part_in, x_sem.at[0], x_sem.at[1], partner)
    cross.start()
    cross.wait()
    size = partial_ref.shape[0] // HALVES
    for half in range(HALVES):
        at = pl.ds(half * size, size)
        summed = partial_ref[at, :].astype(jnp.float32) + part_in[at, :].astype(jnp.float32)
        stream = (residual_ref[at, :].astype(jnp.float32) + summed).astype(jnp.bfloat16)
        stream_ref[at, :] = stream
        out_ref[row, at, :] = normalize(stream, gain_ref[...])

    def piece(source, half, which):
        return out_ref.at[ring_row(place + source, chips, which), pl.ds(half * size, size)]

    def hop(way, distance, half):
        source = -distance if way == 0 else distance
        back = source + (1 if way == 0 else -1)
        return remote(piece(back, half, core), piece(back, half, core),
                      send.at[way, distance - 1, half], recv.at[way, distance - 1, half], ways[way])

    def landed(way, distance, half):
        source = -distance if way == 0 else distance
        return remote(piece(source, half, core), piece(source, half, core),
                      send.at[way, distance - 1, half], recv.at[way, distance - 1, half], ways[way])

    def pass_on(way, distance, half, which):
        source = -distance if way == 0 else distance
        return remote(piece(source, half, which), piece(source, half, which),
                      sib_send.at[way, distance, half], sib_recv.at[way, distance, half], sibling)

    sent = []
    for half in range(HALVES):
        for way in range(2):
            if half in ring_halves(1, half_way, way):
                copy = hop(way, 1, half)
                copy.start()
                sent.append(copy)
        copy = pass_on(0, 0, half, core)
        copy.start()
        sent.append(copy)
    for distance in range(1, half_way + 1):
        for half in range(HALVES):
            for way in range(2):
                if half not in ring_halves(distance, half_way, way):
                    continue
                landed(way, distance, half).wait_recv()
                if distance < half_way and half in ring_halves(distance + 1, half_way, way):
                    copy = hop(way, distance + 1, half)
                    copy.start()
                    sent.append(copy)
                copy = pass_on(way, distance, half, core)
                copy.start()
                sent.append(copy)
    for half in range(HALVES):
        pass_on(0, 0, half, 1 - core).wait_recv()
    for distance in range(1, half_way + 1):
        for half in range(HALVES):
            for way in range(2):
                if half in ring_halves(distance, half_way, way):
                    pass_on(way, distance, half, 1 - core).wait_recv()
    for copy in sent:
        copy.wait_send()


def spread(partial, residual, gain, rows):
    half_way = rows // 4
    return pl.pallas_call(
        lambda *refs: spread_kernel(rows, *refs),
        out_shape=(
            jax.ShapeDtypeStruct(residual.shape, jnp.bfloat16),
            jax.ShapeDtypeStruct((rows, *residual.shape), jnp.bfloat16),
        ),
        in_specs=[VMEM] * 3,
        out_specs=(VMEM, VMEM),
        scratch_shapes=[
            pltpu.VMEM(residual.shape, jnp.bfloat16),
            pltpu.SemaphoreType.DMA((2,)),
            pltpu.SemaphoreType.DMA((2, half_way, HALVES)),
            pltpu.SemaphoreType.DMA((2, half_way, HALVES)),
            pltpu.SemaphoreType.DMA((2, half_way + 1, HALVES)),
            pltpu.SemaphoreType.DMA((2, half_way + 1, HALVES)),
        ],
        compiler_params=pltpu.CompilerParams(
            collective_id=2, has_side_effects=True, vmem_limit_bytes=VMEM_BYTES
        ),
        name="spread",
    )(partial, residual, gain.reshape(1, -1))


def fold_kernel(rows, part_ref, out_ref, sib_buf, ring_in, ring_out, x_out, x_in,
                x_sem, send, recv, sib_send, sib_recv):
    chips = rows // 2
    half_way = chips // 2
    row = lax.axis_index("row")
    col = lax.axis_index("col")
    core = lax.rem(row, 2)
    place = ring_place(row, chips)
    sibling = {"row": row + 1 - 2 * core}
    partner = {"col": 1 - col}
    ways = [{"row": ring_row(place + 1, chips, core)}, {"row": ring_row(place - 1, chips, core)}]
    greet([sibling, partner] + ways)
    order = [half_way]
    for distance in range(half_way - 1, 0, -1):
        order += [distance, chips - distance]
    order.append(0)
    shared = {}
    for offset in order:
        copy = remote(part_ref.at[ring_row(place + offset, chips, 1 - core)], sib_buf.at[offset],
                      sib_send.at[offset], sib_recv.at[offset], sibling)
        copy.start()
        shared[offset] = copy
    size = part_ref.shape[1] // HALVES
    seen = set()

    def own(offset, half):
        if offset not in seen:
            shared[offset].wait_recv()
            seen.add(offset)
        at = pl.ds(half * size, size)
        return part_ref[ring_row(place + offset, chips, core), at, :].astype(
            jnp.float32
        ) + sib_buf[offset, at, :].astype(jnp.float32)

    def hop(way, distance, half):
        at = pl.ds(half * size, size)
        return remote(ring_out.at[way, distance - 1, at], ring_in.at[way, distance - 1, at],
                      send.at[way, distance - 1, half], recv.at[way, distance - 1, half], ways[way])

    def arrived(way, distance, half):
        hop(way, distance, half).wait_recv()
        return ring_in[way, distance - 1, pl.ds(half * size, size), :].astype(jnp.float32)

    sent = []
    for distance in range(half_way, 0, -1):
        for half in range(HALVES):
            for way in range(2):
                if half not in ring_halves(distance, half_way, way):
                    continue
                value = own(distance if way == 0 else chips - distance, half)
                if distance < half_way and half in ring_halves(distance + 1, half_way, way):
                    value = value + arrived(way, distance + 1, half)
                ring_out[way, distance - 1, pl.ds(half * size, size), :] = value.astype(jnp.bfloat16)
                copy = hop(way, distance, half)
                copy.start()
                sent.append(copy)
    width = out_ref.shape[1]
    crosses = []
    for half in range(HALVES):
        at = pl.ds(half * size, size)
        value = own(0, half)
        for way in range(2):
            if half in ring_halves(1, half_way, way):
                value = value + arrived(way, 1, half)
        low, high = value[:, :width], value[:, width:]
        x_out[at, :] = jnp.where(col == 0, high, low).astype(jnp.bfloat16)
        out_ref[at, :] = jnp.where(col == 0, low, high)
        copy = remote(x_out.at[at], x_in.at[at], x_sem.at[0, half], x_sem.at[1, half], partner)
        copy.start()
        crosses.append(copy)
    for half in range(HALVES):
        at = pl.ds(half * size, size)
        crosses[half].wait()
        out_ref[at, :] += x_in[at, :].astype(jnp.float32)
    for copy in sent:
        copy.wait_send()
    for offset in order:
        shared[offset].wait_send()


def fold(part, rows, width):
    half_way = rows // 4
    block = part.shape[1:]
    return pl.pallas_call(
        lambda *refs: fold_kernel(rows, *refs),
        out_shape=jax.ShapeDtypeStruct((block[0], width), jnp.float32),
        in_specs=[VMEM],
        out_specs=VMEM,
        scratch_shapes=[
            pltpu.VMEM((rows // 2, *block), jnp.bfloat16),
            pltpu.VMEM((2, half_way, *block), jnp.bfloat16),
            pltpu.VMEM((2, half_way, *block), jnp.bfloat16),
            pltpu.VMEM((block[0], width), jnp.bfloat16),
            pltpu.VMEM((block[0], width), jnp.bfloat16),
            pltpu.SemaphoreType.DMA((2, HALVES)),
            pltpu.SemaphoreType.DMA((2, half_way, HALVES)),
            pltpu.SemaphoreType.DMA((2, half_way, HALVES)),
            pltpu.SemaphoreType.DMA((rows // 2,)),
            pltpu.SemaphoreType.DMA((rows // 2,)),
        ],
        compiler_params=pltpu.CompilerParams(
            collective_id=3, has_side_effects=True, vmem_limit_bytes=VMEM_BYTES
        ),
        name="fold",
    )(part)


def local(
    residual,
    query_states,
    key_states,
    value_states,
    segment_ids,
    sink_logits,
    w_out,
    norm_gain,
    expert_ids,
    route_weight,
    w_gate_up,
    w_down,
):
    tok_rows = query_states.shape[0]
    row_count = lax.axis_size("row")
    col_count = lax.axis_size("col")
    row_index = lax.axis_index("row")
    col_index = lax.axis_index("col")
    local_heads = sink_logits.shape[0]
    group_size = HEADS // KV_HEADS
    if local_heads >= group_size:
        kv_count = local_heads // group_size
        kv_first = col_index * kv_count
    else:
        kv_count = 1
        kv_first = col_index * local_heads // group_size
    kv_width = kv_count * HEAD_DIM
    own_keys = lax.dynamic_slice_in_dim(key_states, kv_first * HEAD_DIM, kv_width, 1)
    own_values = lax.dynamic_slice_in_dim(value_states, kv_first * HEAD_DIM, kv_width, 1)
    shift_count = (WINDOW + tok_rows - 2) // tok_rows
    block_bytes = 2 * residual.shape[0] * residual.shape[1]
    in_kernels = (
        col_count == 2 and row_count % 4 == 0 and row_count >= 8
        and 4 * row_count * block_bytes < VMEM_BYTES
    )
    routing = jnp.concatenate([expert_ids.astype(jnp.float32), route_weight], 1).T
    key_parts = []
    value_parts = []
    segment_parts = []
    start_parts = []
    if in_kernels:
        own_pair = jnp.concatenate([own_keys, own_values], 1)
        meta = jnp.concatenate(
            [routing, jnp.broadcast_to(segment_ids.astype(jnp.float32)[None], (8, tok_rows))], 0
        )
        pairs, metas = halo(own_pair, meta, row_count, shift_count)
        routing = metas[:, : 2 * TOP]
        all_segments = metas[:, 2 * TOP].astype(jnp.int32)
    else:
        routing = lax.all_gather(routing, "row", axis=0, tiled=False)
    for offset in range(shift_count, 0, -1):
        if in_kernels:
            before = lax.rem(row_index - offset + row_count, row_count)
            arrived = (
                pairs[offset - 1][:, :kv_width],
                pairs[offset - 1][:, kv_width:],
                lax.dynamic_index_in_dim(all_segments, before, 0, keepdims=False),
            )
        else:
            arrived = shifted((own_keys, own_values, segment_ids), "row", offset)
        key_parts.append(arrived[0])
        value_parts.append(arrived[1])
        segment_parts.append(arrived[2])
        start_parts.append((row_index - offset) * tok_rows)
    key_parts.append(own_keys)
    value_parts.append(own_values)
    segment_parts.append(segment_ids)
    start_parts.append(row_index * tok_rows)
    key_groups = jnp.concatenate(key_parts, 0).reshape(-1, kv_count, HEAD_DIM)
    value_groups = jnp.concatenate(value_parts, 0).reshape(-1, kv_count, HEAD_DIM)
    key_segments = jnp.concatenate(segment_parts, 0)
    positions = jnp.arange(tok_rows, dtype=jnp.int32)
    key_position = jnp.concatenate([start + positions for start in start_parts], 0)
    query_position = row_index * tok_rows + positions
    allowed = (key_position[None, :] >= 0) & (key_position[None, :] <= query_position[:, None])
    allowed = allowed & (key_position[None, :] > query_position[:, None] - WINDOW)
    allowed = allowed & (key_segments[None, :] == segment_ids[:, None])
    query_groups = query_states.reshape(tok_rows, kv_count, local_heads // kv_count, HEAD_DIM)
    sink_groups = sink_logits.reshape(kv_count, local_heads // kv_count, 1, 1)
    attended = attend(query_groups, key_groups, value_groups, allowed, sink_groups).reshape(
        tok_rows, local_heads * HEAD_DIM
    )
    partial_value = jnp.dot(attended, w_out, preferred_element_type=jnp.float32)
    feature_count = residual.shape[1] // col_count
    experts_all = w_gate_up.shape[0] * row_count
    slot_cap = max(2, 2 * TOP * tok_rows // experts_all)
    names_mine = routing[:, :TOP] == row_index.astype(jnp.float32)
    mine = jnp.any(names_mine, axis=1)
    weight = jnp.sum(jnp.where(names_mine, routing[:, TOP:], 0.0), axis=1)
    slot_of = jnp.cumsum(mine.astype(jnp.int32), axis=1) - 1
    slots = jnp.arange(slot_cap, dtype=jnp.int32)
    chosen = mine[:, None, :] & (slot_of[:, None, :] == slots[None, :, None])
    selector = chosen.astype(jnp.bfloat16)
    combine = jnp.where(chosen, weight[:, None, :], 0.0)
    expert_gate_up = w_gate_up[0]
    expert_down = w_down[0]
    partial_value = partial_value.astype(jnp.bfloat16)
    if in_kernels:
        stream, gathered = spread(partial_value, residual, norm_gain, row_count)
    else:
        summed = lax.psum(partial_value, "col").astype(jnp.float32)
        stream = (residual.astype(jnp.float32) + summed).astype(jnp.bfloat16)
        gathered = lax.all_gather(normalize(stream, norm_gain), "row", axis=0, tiled=False)
    stream_part = lax.dynamic_slice_in_dim(stream, col_index * feature_count, feature_count, 1)
    packed = jnp.einsum(
        "nst,ntd->nsd", selector, gathered, preferred_element_type=jnp.float32
    ).astype(jnp.bfloat16).reshape(row_count * slot_cap, -1)
    gate = jnp.dot(packed, expert_gate_up[0], preferred_element_type=jnp.float32)
    up = jnp.dot(packed, expert_gate_up[1], preferred_element_type=jnp.float32)
    active = ((up + 1.0) * gate * jax.nn.sigmoid(1.702 * gate)).astype(jnp.bfloat16)
    expert_partial = jnp.dot(active, expert_down, preferred_element_type=jnp.float32)
    scaled = expert_partial.reshape(row_count, slot_cap, -1) * jnp.sum(combine, 2)[:, :, None]
    mixed = jnp.einsum(
        "nst,nsd->ntd", selector, scaled.astype(jnp.bfloat16), preferred_element_type=jnp.float32
    ).astype(jnp.bfloat16)
    if in_kernels:
        mixed = fold(mixed, row_count, feature_count)
    else:
        mixed = mixed.reshape(row_count * tok_rows, -1)
        mixed = lax.psum_scatter(mixed, "row", scatter_dimension=0, tiled=True)
        mixed = lax.psum_scatter(mixed, "col", scatter_dimension=1, tiled=True)
    return (stream_part.astype(jnp.float32) + mixed.astype(jnp.float32)).astype(jnp.bfloat16)


def solution(mesh):
    in_specs = (
        P("row", None),
        P("row", "col"),
        P("row", None),
        P("row", None),
        P("row"),
        P("col"),
        P("col", None),
        P(),
        P("row", None),
        P("row", None),
        P("row", None, None, "col"),
        P("row", "col", None),
    )
    out_specs = P("row", "col")
    return jax.shard_map(local, mesh=mesh, in_specs=in_specs, out_specs=out_specs, check_vma=False)
```

```python
import jax
import jax.numpy as jnp
from jax import lax
from jax.experimental import pallas as pl
from jax.experimental.pallas import tpu as pltpu
from jax.sharding import PartitionSpec as P

HEADS = 64
KV_HEADS = 8
HEAD_DIM = 64
WINDOW = 128
TOP = 4


epsilon = 1e-05
masked_score = -1e30


def shifted(shard, axis, by):
    size = lax.axis_size(axis)
    pairs = [(i, i + by) for i in range(size) if 0 <= i + by < size]
    return lax.ppermute(shard, axis, pairs)


def normalize(stream_rows, norm_gain):
    values32 = stream_rows.astype(jnp.float32)
    square_mean = jnp.mean(values32 * values32, axis=-1, keepdims=True)
    return (values32 * lax.rsqrt(square_mean + epsilon) * norm_gain).astype(jnp.bfloat16)


def attend(query_groups, key_groups, value_groups, allowed, sink_groups):
    scores = jnp.einsum(
        "tgjd,lgd->gjtl", query_groups, key_groups, preferred_element_type=jnp.float32
    )
    scores = scores * query_groups.shape[-1] ** (-0.5)
    scores = jnp.where(allowed[None, None], scores, masked_score)
    peak_score = jnp.maximum(jnp.max(scores, axis=-1, keepdims=True), sink_groups)
    numerator = jnp.exp(scores - peak_score)
    denominator = jnp.exp(sink_groups - peak_score) + jnp.sum(numerator, axis=-1, keepdims=True)
    weights = (numerator / denominator).astype(jnp.bfloat16)
    return jnp.einsum(
        "gjtl,lgd->tgjd", weights, value_groups, preferred_element_type=jnp.float32
    ).astype(jnp.bfloat16)


MESH = pl.DeviceIdType.MESH
VMEM = pl.BlockSpec(memory_space=pltpu.VMEM)
PIECES = 4
VMEM_BYTES = 60 * 1024 * 1024


def ring_place(row, chips):
    chip = lax.div(row, 2)
    along = lax.div(chip, 2)
    return jnp.where(lax.rem(chip, 2) == 0, along, chips - 1 - along)


def ring_row(place, chips, core):
    place = lax.rem(place + chips, chips)
    chip = jnp.where(place < chips // 2, 2 * place, 2 * (chips - 1 - place) + 1)
    return 2 * chip + core


def greet(devices):
    barrier = pltpu.get_barrier_semaphore()
    for device in devices:
        pl.semaphore_signal(barrier, inc=1, device_id=device, device_id_type=MESH)
    pl.semaphore_wait(barrier, len(devices))


def remote(src, dst, send, recv, device):
    return pltpu.make_async_remote_copy(
        src_ref=src, dst_ref=dst, send_sem=send, recv_sem=recv, device_id=device,
        device_id_type=MESH,
    )


def halo_kernel(rows, shifts, kv_ref, meta_ref, kv_out, meta_out, kv_send, kv_recv, m_send, m_recv, l_sem):
    row = lax.axis_index("row")
    others = [{"row": lax.rem(row + step, rows)} for step in range(1, rows)]
    greet(others)
    copies = []
    for shift in range(1, shifts + 1):
        copies.append(
            remote(kv_ref, kv_out.at[shift - 1], kv_send.at[shift - 1], kv_recv.at[shift - 1],
                   others[shift - 1])
        )
    for step in range(1, rows):
        copies.append(
            remote(meta_ref, meta_out.at[row], m_send.at[step - 1], m_recv.at[step - 1],
                   others[step - 1])
        )
    for copy in copies:
        copy.start()
    mine = pltpu.make_async_copy(meta_ref, meta_out.at[row], l_sem)
    mine.start()
    for shift in range(1, shifts + 1):
        copies[shift - 1].wait()
    for step in range(1, rows):
        copies[shifts + step - 1].wait_send()
        source = lax.rem(row - step + rows, rows)
        remote(meta_ref, meta_out.at[source], m_send.at[step - 1], m_recv.at[step - 1],
               others[step - 1]).wait_recv()
    mine.wait()


def halo(kv, meta, rows, shifts):
    return pl.pallas_call(
        lambda *refs: halo_kernel(rows, shifts, *refs),
        out_shape=(
            jax.ShapeDtypeStruct((shifts, *kv.shape), kv.dtype),
            jax.ShapeDtypeStruct((rows, *meta.shape), meta.dtype),
        ),
        in_specs=[VMEM] * 2,
        out_specs=(VMEM, VMEM),
        scratch_shapes=[
            pltpu.SemaphoreType.DMA((shifts,)),
            pltpu.SemaphoreType.DMA((shifts,)),
            pltpu.SemaphoreType.DMA((rows,)),
            pltpu.SemaphoreType.DMA((rows,)),
            pltpu.SemaphoreType.DMA,
        ],
        compiler_params=pltpu.CompilerParams(
            collective_id=1, has_side_effects=True, vmem_limit_bytes=16 * 1024 * 1024
        ),
        name="halo",
    )(kv, meta)


def ring_pieces(distance, half_way, way):
    if distance < half_way:
        return [1, 2, 0]
    return [1, 0] if way == 0 else [2]


def piece_rows(index, size):
    col = lax.axis_index("col")
    start = (index + col * (PIECES - 1 - 2 * index)) * size
    return pl.ds(pl.multiple_of(start, size), size)


def spread_kernel(rows, partial_ref, residual_ref, gain_ref, stream_ref, out_ref, part_in,
                  x_sem, send, recv, over_send, over_recv, sib_send, sib_recv):
    chips = rows // 2
    half_way = chips // 2
    row = lax.axis_index("row")
    col = lax.axis_index("col")
    core = lax.rem(row, 2)
    place = ring_place(row, chips)
    sibling = {"row": row + 1 - 2 * core}
    partner = {"col": 1 - col}
    ways = [{"row": ring_row(place + 1, chips, core)}, {"row": ring_row(place - 1, chips, core)}]
    greet([sibling, partner] + ways)
    cross = remote(partial_ref, part_in, x_sem.at[0], x_sem.at[1], partner)
    cross.start()
    cross.wait()
    size = partial_ref.shape[0] // PIECES
    for half in range(2):
        at = pl.ds(half * 2 * size, 2 * size)
        summed = partial_ref[at, :].astype(jnp.float32) + part_in[at, :].astype(jnp.float32)
        stream = (residual_ref[at, :].astype(jnp.float32) + summed).astype(jnp.bfloat16)
        stream_ref[at, :] = stream
        out_ref[row, at, :] = normalize(stream, gain_ref[...])

    def part(offset, index, which):
        return out_ref.at[ring_row(place + offset, chips, which), piece_rows(index, size)]

    def offset_of(way, distance):
        return -distance if way == 0 else distance

    def hop(way, distance, index, sending):
        at = part(offset_of(way, distance - 1 if sending else distance), index, core)
        return remote(at, at, send.at[way, distance - 1, index], recv.at[way, distance - 1, index],
                      ways[way])

    def over(way, distance, sending):
        at = part(offset_of(way, distance), 0 if sending else PIECES - 1, core)
        return remote(at, at, over_send.at[way, distance - 1], over_recv.at[way, distance - 1],
                      partner)

    def pass_on(way, distance, index, which):
        at = part(offset_of(way, distance), index, which)
        return remote(at, at, sib_send.at[way, distance, index], sib_recv.at[way, distance, index],
                      sibling)

    sent = []

    def go(copy):
        copy.start()
        sent.append(copy)

    for index in [1, 2, 0]:
        for way in range(2):
            if index in ring_pieces(1, half_way, way):
                go(hop(way, 1, index, True))
    mine = out_ref.at[row]
    theirs = out_ref.at[row + 1 - 2 * core]
    go(remote(mine, mine, x_sem.at[2], x_sem.at[3], sibling))
    for distance in range(1, half_way + 1):
        for index in [1, 2, 0]:
            for way in range(2):
                if index not in ring_pieces(distance, half_way, way):
                    continue
                hop(way, distance, index, False).wait_recv()
                if distance < half_way and index in ring_pieces(distance + 1, half_way, way):
                    go(hop(way, distance + 1, index, True))
                if index == 0:
                    go(over(way, distance, True))
                go(pass_on(way, distance, index, core))
        for way in range(2):
            if distance > 1 and 0 in ring_pieces(distance - 1, half_way, way):
                over(way, distance - 1, False).wait_recv()
                go(pass_on(way, distance - 1, PIECES - 1, core))
    for way in range(2):
        if 0 in ring_pieces(half_way, half_way, way):
            over(way, half_way, False).wait_recv()
            go(pass_on(way, half_way, PIECES - 1, core))
    remote(theirs, theirs, x_sem.at[2], x_sem.at[3], sibling).wait_recv()
    for distance in range(1, half_way + 1):
        for way in range(2):
            indices = list(ring_pieces(distance, half_way, way))
            for index in indices + ([PIECES - 1] if 0 in indices else []):
                pass_on(way, distance, index, 1 - core).wait_recv()
    for copy in sent:
        copy.wait_send()


def spread(partial, residual, gain, rows):
    half_way = rows // 4
    return pl.pallas_call(
        lambda *refs: spread_kernel(rows, *refs),
        out_shape=(
            jax.ShapeDtypeStruct(residual.shape, jnp.bfloat16),
            jax.ShapeDtypeStruct((rows, *residual.shape), jnp.bfloat16),
        ),
        in_specs=[VMEM] * 3,
        out_specs=(VMEM, VMEM),
        scratch_shapes=[
            pltpu.VMEM(residual.shape, jnp.bfloat16),
            pltpu.SemaphoreType.DMA((4,)),
            pltpu.SemaphoreType.DMA((2, half_way, PIECES)),
            pltpu.SemaphoreType.DMA((2, half_way, PIECES)),
            pltpu.SemaphoreType.DMA((2, half_way)),
            pltpu.SemaphoreType.DMA((2, half_way)),
            pltpu.SemaphoreType.DMA((2, half_way + 1, PIECES)),
            pltpu.SemaphoreType.DMA((2, half_way + 1, PIECES)),
        ],
        compiler_params=pltpu.CompilerParams(
            collective_id=2, has_side_effects=True, vmem_limit_bytes=VMEM_BYTES // 4
        ),
        name="spread",
    )(partial, residual, gain.reshape(1, -1))


def fold_kernel(rows, part_ref, out_ref, sib_buf, ring_in, ring_out, over_out, over_in, x_out, x_in,
                x_sem, send, recv, over_send, over_recv, sib_send, sib_recv):
    chips = rows // 2
    half_way = chips // 2
    row = lax.axis_index("row")
    col = lax.axis_index("col")
    core = lax.rem(row, 2)
    place = ring_place(row, chips)
    sibling = {"row": row + 1 - 2 * core}
    partner = {"col": 1 - col}
    ways = [{"row": ring_row(place + 1, chips, core)}, {"row": ring_row(place - 1, chips, core)}]
    greet([sibling, partner] + ways)
    order = [half_way]
    for distance in range(half_way - 1, 0, -1):
        order += [distance, chips - distance]
    order.append(0)
    shared = {}
    for offset in order:
        copy = remote(part_ref.at[ring_row(place + offset, chips, 1 - core)], sib_buf.at[offset],
                      sib_send.at[offset], sib_recv.at[offset], sibling)
        copy.start()
        shared[offset] = copy
    size = part_ref.shape[1] // PIECES
    seen = set()

    def own(offset, index):
        if offset not in seen:
            shared[offset].wait_recv()
            seen.add(offset)
        at = piece_rows(index, size)
        return part_ref[ring_row(place + offset, chips, core), at, :].astype(
            jnp.float32
        ) + sib_buf[offset, at, :].astype(jnp.float32)

    def hop(way, distance, index):
        at = pl.ds(index * size, size)
        return remote(ring_out.at[way, distance - 1, at], ring_in.at[way, distance - 1, at],
                      send.at[way, distance - 1, index], recv.at[way, distance - 1, index],
                      ways[way])

    def arrived(way, distance, index):
        hop(way, distance, index).wait_recv()
        return ring_in[way, distance - 1, pl.ds(index * size, size), :].astype(jnp.float32)

    def over(offset):
        return remote(over_out.at[offset], over_in.at[offset], over_send.at[offset],
                      over_recv.at[offset], partner)

    sent = []

    def go(copy):
        copy.start()
        sent.append(copy)

    for distance in range(half_way, 0, -1):
        for offset in sorted({distance, chips - distance}):
            over_out[offset] = own(offset, PIECES - 1).astype(jnp.bfloat16)
            go(over(offset))
        for index in [1, 2, 0]:
            for way in range(2):
                if index not in ring_pieces(distance, half_way, way):
                    continue
                offset = distance if way == 0 else chips - distance
                value = own(offset, index)
                if index == 0:
                    over(offset).wait_recv()
                    value = value + over_in[offset].astype(jnp.float32)
                if distance < half_way and index in ring_pieces(distance + 1, half_way, way):
                    value = value + arrived(way, distance + 1, index)
                ring_out[way, distance - 1, pl.ds(index * size, size), :] = value.astype(
                    jnp.bfloat16
                )
                go(hop(way, distance, index))
    width = out_ref.shape[1]
    crosses = []
    for index in [3, 1, 2, 0]:
        at = piece_rows(index, size)
        value = own(0, index)
        for way in range(2):
            if index in ring_pieces(1, half_way, way):
                value = value + arrived(way, 1, index)
        low, high = value[:, :width], value[:, width:]
        x_out[at, :] = jnp.where(col == 0, high, low).astype(jnp.bfloat16)
        out_ref[at, :] = jnp.where(col == 0, low, high)
        copy = remote(x_out.at[at], x_in.at[at], x_sem.at[0, index], x_sem.at[1, index], partner)
        go(copy)
    for index in [0, 2, 1, 3]:
        at = piece_rows(index, size)
        named = PIECES - 1 - index
        remote(x_out.at[at], x_in.at[at], x_sem.at[0, named], x_sem.at[1, named],
               partner).wait_recv()
        out_ref[at, :] += x_in[at, :].astype(jnp.float32)
    for copy in sent:
        copy.wait_send()
    for offset in order:
        shared[offset].wait_send()


def fold(part, rows, width):
    half_way = rows // 4
    block = part.shape[1:]
    return pl.pallas_call(
        lambda *refs: fold_kernel(rows, *refs),
        out_shape=jax.ShapeDtypeStruct((block[0], width), jnp.float32),
        in_specs=[VMEM],
        out_specs=VMEM,
        scratch_shapes=[
            pltpu.VMEM((rows // 2, *block), jnp.bfloat16),
            pltpu.VMEM((2, half_way, *block), jnp.bfloat16),
            pltpu.VMEM((2, half_way, *block), jnp.bfloat16),
            pltpu.VMEM((rows // 2, block[0] // PIECES, block[1]), jnp.bfloat16),
            pltpu.VMEM((rows // 2, block[0] // PIECES, block[1]), jnp.bfloat16),
            pltpu.VMEM((block[0], width), jnp.bfloat16),
            pltpu.VMEM((block[0], width), jnp.bfloat16),
            pltpu.SemaphoreType.DMA((2, PIECES)),
            pltpu.SemaphoreType.DMA((2, half_way, PIECES)),
            pltpu.SemaphoreType.DMA((2, half_way, PIECES)),
            pltpu.SemaphoreType.DMA((rows // 2,)),
            pltpu.SemaphoreType.DMA((rows // 2,)),
            pltpu.SemaphoreType.DMA((rows // 2,)),
            pltpu.SemaphoreType.DMA((rows // 2,)),
        ],
        compiler_params=pltpu.CompilerParams(
            collective_id=3, has_side_effects=True, vmem_limit_bytes=VMEM_BYTES // 5 * 2
        ),
        name="fold",
    )(part)


def local(
    residual,
    query_states,
    key_states,
    value_states,
    segment_ids,
    sink_logits,
    w_out,
    norm_gain,
    expert_ids,
    route_weight,
    w_gate_up,
    w_down,
):
    tok_rows = query_states.shape[0]
    row_count = lax.axis_size("row")
    col_count = lax.axis_size("col")
    row_index = lax.axis_index("row")
    col_index = lax.axis_index("col")
    local_heads = sink_logits.shape[0]
    group_size = HEADS // KV_HEADS
    if local_heads >= group_size:
        kv_count = local_heads // group_size
        kv_first = col_index * kv_count
    else:
        kv_count = 1
        kv_first = col_index * local_heads // group_size
    kv_width = kv_count * HEAD_DIM
    own_keys = lax.dynamic_slice_in_dim(key_states, kv_first * HEAD_DIM, kv_width, 1)
    own_values = lax.dynamic_slice_in_dim(value_states, kv_first * HEAD_DIM, kv_width, 1)
    shift_count = (WINDOW + tok_rows - 2) // tok_rows
    block_bytes = 2 * residual.shape[0] * residual.shape[1]
    in_kernels = (
        col_count == 2 and row_count % 4 == 0 and row_count >= 8 and tok_rows % 64 == 0
        and 4 * row_count * block_bytes < VMEM_BYTES
    )
    routing = jnp.concatenate([expert_ids.astype(jnp.float32), route_weight], 1).T
    key_parts = []
    value_parts = []
    segment_parts = []
    start_parts = []
    if in_kernels:
        own_pair = jnp.concatenate([own_keys, own_values], 1)
        meta = jnp.concatenate(
            [routing, jnp.broadcast_to(segment_ids.astype(jnp.float32)[None], (8, tok_rows))], 0
        )
        pairs, metas = halo(own_pair, meta, row_count, shift_count)
        routing = metas[:, : 2 * TOP]
        all_segments = metas[:, 2 * TOP].astype(jnp.int32)
    else:
        routing = lax.all_gather(routing, "row", axis=0, tiled=False)
    for offset in range(shift_count, 0, -1):
        if in_kernels:
            before = lax.rem(row_index - offset + row_count, row_count)
            arrived = (
                pairs[offset - 1][:, :kv_width],
                pairs[offset - 1][:, kv_width:],
                lax.dynamic_index_in_dim(all_segments, before, 0, keepdims=False),
            )
        else:
            arrived = shifted((own_keys, own_values, segment_ids), "row", offset)
        key_parts.append(arrived[0])
        value_parts.append(arrived[1])
        segment_parts.append(arrived[2])
        start_parts.append((row_index - offset) * tok_rows)
    key_parts.append(own_keys)
    value_parts.append(own_values)
    segment_parts.append(segment_ids)
    start_parts.append(row_index * tok_rows)
    key_groups = jnp.concatenate(key_parts, 0).reshape(-1, kv_count, HEAD_DIM)
    value_groups = jnp.concatenate(value_parts, 0).reshape(-1, kv_count, HEAD_DIM)
    key_segments = jnp.concatenate(segment_parts, 0)
    positions = jnp.arange(tok_rows, dtype=jnp.int32)
    key_position = jnp.concatenate([start + positions for start in start_parts], 0)
    query_position = row_index * tok_rows + positions
    allowed = (key_position[None, :] >= 0) & (key_position[None, :] <= query_position[:, None])
    allowed = allowed & (key_position[None, :] > query_position[:, None] - WINDOW)
    allowed = allowed & (key_segments[None, :] == segment_ids[:, None])
    query_groups = query_states.reshape(tok_rows, kv_count, local_heads // kv_count, HEAD_DIM)
    sink_groups = sink_logits.reshape(kv_count, local_heads // kv_count, 1, 1)
    attended = attend(query_groups, key_groups, value_groups, allowed, sink_groups).reshape(
        tok_rows, local_heads * HEAD_DIM
    )
    partial_value = jnp.dot(attended, w_out, preferred_element_type=jnp.float32)
    feature_count = residual.shape[1] // col_count
    experts_all = w_gate_up.shape[0] * row_count
    slot_cap = max(2, 2 * TOP * tok_rows // experts_all)
    names_mine = routing[:, :TOP] == row_index.astype(jnp.float32)
    mine = jnp.any(names_mine, axis=1)
    weight = jnp.sum(jnp.where(names_mine, routing[:, TOP:], 0.0), axis=1)
    slot_of = jnp.cumsum(mine.astype(jnp.int32), axis=1) - 1
    slots = jnp.arange(slot_cap, dtype=jnp.int32)
    chosen = mine[:, None, :] & (slot_of[:, None, :] == slots[None, :, None])
    selector = chosen.astype(jnp.bfloat16)
    combine = jnp.where(chosen, weight[:, None, :], 0.0)
    expert_gate_up = w_gate_up[0]
    expert_down = w_down[0]
    partial_value = partial_value.astype(jnp.bfloat16)
    if in_kernels:
        stream, gathered = spread(partial_value, residual, norm_gain, row_count)
    else:
        summed = lax.psum(partial_value, "col").astype(jnp.float32)
        stream = (residual.astype(jnp.float32) + summed).astype(jnp.bfloat16)
        gathered = lax.all_gather(normalize(stream, norm_gain), "row", axis=0, tiled=False)
    stream_part = lax.dynamic_slice_in_dim(stream, col_index * feature_count, feature_count, 1)
    packed = jnp.einsum(
        "nst,ntd->nsd", selector, gathered, preferred_element_type=jnp.float32
    ).astype(jnp.bfloat16).reshape(row_count * slot_cap, -1)
    gate = jnp.dot(packed, expert_gate_up[0], preferred_element_type=jnp.float32)
    up = jnp.dot(packed, expert_gate_up[1], preferred_element_type=jnp.float32)
    active = ((up + 1.0) * gate * jax.nn.sigmoid(1.702 * gate)).astype(jnp.bfloat16)
    expert_partial = jnp.dot(active, expert_down, preferred_element_type=jnp.float32)
    scaled = expert_partial.reshape(row_count, slot_cap, -1) * jnp.sum(combine, 2)[:, :, None]
    mixed = jnp.einsum(
        "nst,nsd->ntd", selector, scaled.astype(jnp.bfloat16), preferred_element_type=jnp.float32
    ).astype(jnp.bfloat16)
    if in_kernels:
        mixed = fold(mixed, row_count, feature_count)
    else:
        mixed = mixed.reshape(row_count * tok_rows, -1)
        mixed = lax.psum_scatter(mixed, "row", scatter_dimension=0, tiled=True)
        mixed = lax.psum_scatter(mixed, "col", scatter_dimension=1, tiled=True)
    return (stream_part.astype(jnp.float32) + mixed.astype(jnp.float32)).astype(jnp.bfloat16)


def solution(mesh):
    in_specs = (
        P("row", None),
        P("row", "col"),
        P("row", None),
        P("row", None),
        P("row"),
        P("col"),
        P("col", None),
        P(),
        P("row", None),
        P("row", None),
        P("row", None, None, "col"),
        P("row", "col", None),
    )
    out_specs = P("row", "col")
    return jax.shard_map(local, mesh=mesh, in_specs=in_specs, out_specs=out_specs, check_vma=False)
```

```python
import jax
import jax.numpy as jnp
from jax import lax
from jax.experimental import pallas as pl
from jax.experimental.pallas import tpu as pltpu
from jax.sharding import PartitionSpec as P

HEADS = 64
KV_HEADS = 8
HEAD_DIM = 64
WINDOW = 128
TOP = 4


epsilon = 1e-05
masked_score = -1e30


def shifted(shard, axis, by):
    size = lax.axis_size(axis)
    pairs = [(i, i + by) for i in range(size) if 0 <= i + by < size]
    return lax.ppermute(shard, axis, pairs)


def normalize(stream_rows, norm_gain):
    values32 = stream_rows.astype(jnp.float32)
    square_mean = jnp.mean(values32 * values32, axis=-1, keepdims=True)
    return (values32 * lax.rsqrt(square_mean + epsilon) * norm_gain).astype(jnp.bfloat16)


def attend(query_groups, key_groups, value_groups, allowed, sink_groups):
    scores = jnp.einsum(
        "tgjd,lgd->gjtl", query_groups, key_groups, preferred_element_type=jnp.float32
    )
    scores = scores * query_groups.shape[-1] ** (-0.5)
    scores = jnp.where(allowed[None, None], scores, masked_score)
    peak_score = jnp.maximum(jnp.max(scores, axis=-1, keepdims=True), sink_groups)
    numerator = jnp.exp(scores - peak_score)
    denominator = jnp.exp(sink_groups - peak_score) + jnp.sum(numerator, axis=-1, keepdims=True)
    weights = (numerator / denominator).astype(jnp.bfloat16)
    return jnp.einsum(
        "gjtl,lgd->tgjd", weights, value_groups, preferred_element_type=jnp.float32
    ).astype(jnp.bfloat16)


MESH = pl.DeviceIdType.MESH
VMEM = pl.BlockSpec(memory_space=pltpu.VMEM)
PIECES = 4
VMEM_BYTES = 60 * 1024 * 1024


def ring_place(row, chips):
    chip = lax.div(row, 2)
    along = lax.div(chip, 2)
    return jnp.where(lax.rem(chip, 2) == 0, along, chips - 1 - along)


def ring_row(place, chips, core):
    place = lax.rem(place + chips, chips)
    chip = jnp.where(place < chips // 2, 2 * place, 2 * (chips - 1 - place) + 1)
    return 2 * chip + core


def greet(devices):
    barrier = pltpu.get_barrier_semaphore()
    for device in devices:
        pl.semaphore_signal(barrier, inc=1, device_id=device, device_id_type=MESH)
    pl.semaphore_wait(barrier, len(devices))


def remote(src, dst, send, recv, device):
    return pltpu.make_async_remote_copy(
        src_ref=src, dst_ref=dst, send_sem=send, recv_sem=recv, device_id=device,
        device_id_type=MESH,
    )


def halo_kernel(rows, shifts, key_ref, value_ref, segment_ref, key_out, value_out, segment_out, send, recv):
    row = lax.axis_index("row")
    col = lax.axis_index("col")
    after = [{"row": lax.rem(row + shift, rows)} for shift in range(1, shifts + 1)]
    before = [{"row": lax.rem(row + rows - shift, rows)} for shift in range(1, shifts + 1)]
    greet(after + before)
    width = key_out.shape[2]
    lanes = pl.ds(pl.multiple_of(col * width, width), width)
    copies = []
    for at in range(shifts):
        for which, (src, dst) in enumerate([
            (segment_ref, segment_out.at[at]),
            (key_ref.at[:, lanes], key_out.at[at]),
            (value_ref.at[:, lanes], value_out.at[at]),
        ]):
            copies.append(remote(src, dst, send.at[at, which], recv.at[at, which], after[at]))
    for copy in copies:
        copy.start()
    for copy in copies:
        copy.wait()


def halo(keys, values, segments, rows, shifts, width):
    tokens = keys.shape[0]
    return pl.pallas_call(
        lambda *refs: halo_kernel(rows, shifts, *refs),
        out_shape=(
            jax.ShapeDtypeStruct((shifts, tokens, width), keys.dtype),
            jax.ShapeDtypeStruct((shifts, tokens, width), values.dtype),
            jax.ShapeDtypeStruct((shifts, 1, tokens), segments.dtype),
        ),
        in_specs=[VMEM] * 3,
        out_specs=(VMEM,) * 3,
        scratch_shapes=[
            pltpu.SemaphoreType.DMA((shifts, 3)),
            pltpu.SemaphoreType.DMA((shifts, 3)),
        ],
        compiler_params=pltpu.CompilerParams(
            collective_id=1, has_side_effects=True, vmem_limit_bytes=16 * 1024 * 1024
        ),
        name="halo",
    )(keys, values, segments.reshape(1, -1))


def ring_pieces(distance, half_way, way):
    if distance < half_way:
        return [1, 2, 0]
    return [1, 0] if way == 0 else [2]


def piece_rows(index, size):
    col = lax.axis_index("col")
    start = (index + col * (PIECES - 1 - 2 * index)) * size
    return pl.ds(pl.multiple_of(start, size), size)


def spread_kernel(rows, partial_ref, residual_ref, gain_ref, meta_ref, stream_ref, out_ref, meta_out, part_in,
                  x_sem, c_send, c_recv, m_send, m_recv, n_send, n_recv, l_sem, send, recv, over_send, over_recv, sib_send, sib_recv):
    chips = rows // 2
    half_way = chips // 2
    row = lax.axis_index("row")
    col = lax.axis_index("col")
    core = lax.rem(row, 2)
    place = ring_place(row, chips)
    sibling = {"row": row + 1 - 2 * core}
    partner = {"col": 1 - col}
    ways = [{"row": ring_row(place + 1, chips, core)}, {"row": ring_row(place - 1, chips, core)}]
    greet([sibling, partner] + ways)
    size = partial_ref.shape[0] // PIECES
    crosses = {}
    for index in [2, 1, 3, 0]:
        at = piece_rows(index, size)
        named = PIECES - 1 - index
        crosses[index] = remote(partial_ref.at[at], part_in.at[at], c_send.at[named],
                                c_recv.at[named], partner)
        crosses[index].start()
    local_meta = pltpu.make_async_copy(meta_ref, meta_out.at[row], l_sem)
    local_meta.start()

    def ready(index):
        at = piece_rows(index, size)
        remote(partial_ref.at[at], part_in.at[at], c_send.at[index], c_recv.at[index],
               partner).wait_recv()
        summed = partial_ref[at, :].astype(jnp.float32) + part_in[at, :].astype(jnp.float32)
        stream = (residual_ref[at, :].astype(jnp.float32) + summed).astype(jnp.bfloat16)
        stream_ref[at, :] = stream
        out_ref[row, at, :] = normalize(stream, gain_ref[...])

    def part(offset, index, which):
        return out_ref.at[ring_row(place + offset, chips, which), piece_rows(index, size)]

    def offset_of(way, distance):
        return -distance if way == 0 else distance

    def hop(way, distance, index, sending):
        at = part(offset_of(way, distance - 1 if sending else distance), index, core)
        return remote(at, at, send.at[way, distance - 1, index], recv.at[way, distance - 1, index],
                      ways[way])

    def over(way, distance, sending):
        at = part(offset_of(way, distance), 0 if sending else PIECES - 1, core)
        return remote(at, at, over_send.at[way, distance - 1], over_recv.at[way, distance - 1],
                      partner)

    def pass_on(way, distance, index, which):
        at = part(offset_of(way, distance), index, which)
        return remote(at, at, sib_send.at[way, distance, index], sib_recv.at[way, distance, index],
                      sibling)

    sent = []

    def go(copy):
        copy.start()
        sent.append(copy)

    for index in [1, 2, 0]:
        ready(index)
        for way in range(2):
            if index in ring_pieces(1, half_way, way):
                go(hop(way, 1, index, True))
    ready(PIECES - 1)
    local_meta.wait()

    def routing_hop(way, distance, sending):
        back = offset_of(way, distance - 1 if sending else distance)
        at = meta_out.at[ring_row(place + back, chips, core)]
        return remote(at, at, m_send.at[way, distance - 1], m_recv.at[way, distance - 1], ways[way])

    def routing_on(way, distance, which):
        at = meta_out.at[ring_row(place + offset_of(way, distance), chips, which)]
        return remote(at, at, n_send.at[way, distance], n_recv.at[way, distance], sibling)

    reach = [half_way, half_way - 1]
    for way in range(2):
        go(routing_hop(way, 1, True))
    go(routing_on(0, 0, core))
    mine = out_ref.at[row]
    theirs = out_ref.at[row + 1 - 2 * core]
    go(remote(mine, mine, x_sem.at[0], x_sem.at[1], sibling))
    for distance in range(1, half_way + 1):
        for index in [1, 2, 0]:
            for way in range(2):
                if index not in ring_pieces(distance, half_way, way):
                    continue
                hop(way, distance, index, False).wait_recv()
                if distance < half_way and index in ring_pieces(distance + 1, half_way, way):
                    go(hop(way, distance + 1, index, True))
                if index == 0:
                    go(over(way, distance, True))
                go(pass_on(way, distance, index, core))
        for way in range(2):
            if distance <= reach[way]:
                routing_hop(way, distance, False).wait_recv()
                if distance < reach[way]:
                    go(routing_hop(way, distance + 1, True))
                go(routing_on(way, distance, core))
        for way in range(2):
            if distance > 1 and 0 in ring_pieces(distance - 1, half_way, way):
                over(way, distance - 1, False).wait_recv()
                go(pass_on(way, distance - 1, PIECES - 1, core))
    for way in range(2):
        if 0 in ring_pieces(half_way, half_way, way):
            over(way, half_way, False).wait_recv()
            go(pass_on(way, half_way, PIECES - 1, core))
    remote(theirs, theirs, x_sem.at[0], x_sem.at[1], sibling).wait_recv()
    for way in range(2):
        for distance in range(way, reach[way] + 1):
            routing_on(way, distance, 1 - core).wait_recv()
    for index in range(PIECES):
        crosses[index].wait_send()
    for distance in range(1, half_way + 1):
        for way in range(2):
            indices = list(ring_pieces(distance, half_way, way))
            for index in indices + ([PIECES - 1] if 0 in indices else []):
                pass_on(way, distance, index, 1 - core).wait_recv()
    for copy in sent:
        copy.wait_send()


def spread(partial, residual, gain, meta, rows):
    half_way = rows // 4
    return pl.pallas_call(
        lambda *refs: spread_kernel(rows, *refs),
        out_shape=(
            jax.ShapeDtypeStruct(residual.shape, jnp.bfloat16),
            jax.ShapeDtypeStruct((rows, *residual.shape), jnp.bfloat16),
            jax.ShapeDtypeStruct((rows, *meta.shape), meta.dtype),
        ),
        in_specs=[VMEM] * 4,
        out_specs=(VMEM,) * 3,
        scratch_shapes=[
            pltpu.VMEM(residual.shape, jnp.bfloat16),
            pltpu.SemaphoreType.DMA((2,)),
            pltpu.SemaphoreType.DMA((PIECES,)),
            pltpu.SemaphoreType.DMA((PIECES,)),
            pltpu.SemaphoreType.DMA((2, half_way)),
            pltpu.SemaphoreType.DMA((2, half_way)),
            pltpu.SemaphoreType.DMA((2, half_way + 1)),
            pltpu.SemaphoreType.DMA((2, half_way + 1)),
            pltpu.SemaphoreType.DMA,
            pltpu.SemaphoreType.DMA((2, half_way, PIECES)),
            pltpu.SemaphoreType.DMA((2, half_way, PIECES)),
            pltpu.SemaphoreType.DMA((2, half_way)),
            pltpu.SemaphoreType.DMA((2, half_way)),
            pltpu.SemaphoreType.DMA((2, half_way + 1, PIECES)),
            pltpu.SemaphoreType.DMA((2, half_way + 1, PIECES)),
        ],
        compiler_params=pltpu.CompilerParams(
            collective_id=2, has_side_effects=True, vmem_limit_bytes=VMEM_BYTES // 4
        ),
        name="spread",
    )(partial, residual, gain.reshape(1, -1), meta)


def fold_kernel(rows, part_ref, out_ref, sib_buf, ring_in, ring_out, over_out, over_in, x_out, x_in,
                x_sem, send, recv, over_send, over_recv, sib_send, sib_recv):
    chips = rows // 2
    half_way = chips // 2
    row = lax.axis_index("row")
    col = lax.axis_index("col")
    core = lax.rem(row, 2)
    place = ring_place(row, chips)
    sibling = {"row": row + 1 - 2 * core}
    partner = {"col": 1 - col}
    ways = [{"row": ring_row(place + 1, chips, core)}, {"row": ring_row(place - 1, chips, core)}]
    greet([sibling, partner] + ways)
    order = [half_way]
    for distance in range(half_way - 1, 0, -1):
        order += [distance, chips - distance]
    order.append(0)
    shared = {}
    for offset in order:
        copy = remote(part_ref.at[ring_row(place + offset, chips, 1 - core)], sib_buf.at[offset],
                      sib_send.at[offset], sib_recv.at[offset], sibling)
        copy.start()
        shared[offset] = copy
    size = part_ref.shape[1] // PIECES
    seen = set()

    def own(offset, index):
        if offset not in seen:
            shared[offset].wait_recv()
            seen.add(offset)
        at = piece_rows(index, size)
        return part_ref[ring_row(place + offset, chips, core), at, :].astype(
            jnp.float32
        ) + sib_buf[offset, at, :].astype(jnp.float32)

    def hop(way, distance, index):
        at = pl.ds(index * size, size)
        return remote(ring_out.at[way, distance - 1, at], ring_in.at[way, distance - 1, at],
                      send.at[way, distance - 1, index], recv.at[way, distance - 1, index],
                      ways[way])

    def arrived(way, distance, index):
        hop(way, distance, index).wait_recv()
        return ring_in[way, distance - 1, pl.ds(index * size, size), :].astype(jnp.float32)

    def over(offset):
        return remote(over_out.at[offset], over_in.at[offset], over_send.at[offset],
                      over_recv.at[offset], partner)

    sent = []

    def go(copy):
        copy.start()
        sent.append(copy)

    for distance in range(half_way, 0, -1):
        for offset in sorted({distance, chips - distance}):
            over_out[offset] = own(offset, PIECES - 1).astype(jnp.bfloat16)
            go(over(offset))
        for index in [1, 2, 0]:
            for way in range(2):
                if index not in ring_pieces(distance, half_way, way):
                    continue
                offset = distance if way == 0 else chips - distance
                value = own(offset, index)
                if index == 0:
                    over(offset).wait_recv()
                    value = value + over_in[offset].astype(jnp.float32)
                if distance < half_way and index in ring_pieces(distance + 1, half_way, way):
                    value = value + arrived(way, distance + 1, index)
                ring_out[way, distance - 1, pl.ds(index * size, size), :] = value.astype(
                    jnp.bfloat16
                )
                go(hop(way, distance, index))
    width = out_ref.shape[1]
    crosses = []
    for index in [3, 1, 2, 0]:
        at = piece_rows(index, size)
        value = own(0, index)
        for way in range(2):
            if index in ring_pieces(1, half_way, way):
                value = value + arrived(way, 1, index)
        low, high = value[:, :width], value[:, width:]
        x_out[at, :] = jnp.where(col == 0, high, low).astype(jnp.bfloat16)
        out_ref[at, :] = jnp.where(col == 0, low, high)
        copy = remote(x_out.at[at], x_in.at[at], x_sem.at[0, index], x_sem.at[1, index], partner)
        go(copy)
    for index in [0, 2, 1, 3]:
        at = piece_rows(index, size)
        named = PIECES - 1 - index
        remote(x_out.at[at], x_in.at[at], x_sem.at[0, named], x_sem.at[1, named],
               partner).wait_recv()
        out_ref[at, :] += x_in[at, :].astype(jnp.float32)
    for copy in sent:
        copy.wait_send()
    for offset in order:
        shared[offset].wait_send()


def fold(part, rows, width):
    half_way = rows // 4
    block = part.shape[1:]
    return pl.pallas_call(
        lambda *refs: fold_kernel(rows, *refs),
        out_shape=jax.ShapeDtypeStruct((block[0], width), jnp.float32),
        in_specs=[VMEM],
        out_specs=VMEM,
        scratch_shapes=[
            pltpu.VMEM((rows // 2, *block), jnp.bfloat16),
            pltpu.VMEM((2, half_way, *block), jnp.bfloat16),
            pltpu.VMEM((2, half_way, *block), jnp.bfloat16),
            pltpu.VMEM((rows // 2, block[0] // PIECES, block[1]), jnp.bfloat16),
            pltpu.VMEM((rows // 2, block[0] // PIECES, block[1]), jnp.bfloat16),
            pltpu.VMEM((block[0], width), jnp.bfloat16),
            pltpu.VMEM((block[0], width), jnp.bfloat16),
            pltpu.SemaphoreType.DMA((2, PIECES)),
            pltpu.SemaphoreType.DMA((2, half_way, PIECES)),
            pltpu.SemaphoreType.DMA((2, half_way, PIECES)),
            pltpu.SemaphoreType.DMA((rows // 2,)),
            pltpu.SemaphoreType.DMA((rows // 2,)),
            pltpu.SemaphoreType.DMA((rows // 2,)),
            pltpu.SemaphoreType.DMA((rows // 2,)),
        ],
        compiler_params=pltpu.CompilerParams(
            collective_id=3, has_side_effects=True, vmem_limit_bytes=VMEM_BYTES // 5 * 2
        ),
        name="fold",
    )(part)


def local(
    residual,
    query_states,
    key_states,
    value_states,
    segment_ids,
    sink_logits,
    w_out,
    norm_gain,
    expert_ids,
    route_weight,
    w_gate_up,
    w_down,
):
    tok_rows = query_states.shape[0]
    row_count = lax.axis_size("row")
    col_count = lax.axis_size("col")
    row_index = lax.axis_index("row")
    col_index = lax.axis_index("col")
    local_heads = sink_logits.shape[0]
    group_size = HEADS // KV_HEADS
    if local_heads >= group_size:
        kv_count = local_heads // group_size
        kv_first = col_index * kv_count
    else:
        kv_count = 1
        kv_first = col_index * local_heads // group_size
    kv_width = kv_count * HEAD_DIM
    own_keys = lax.dynamic_slice_in_dim(key_states, kv_first * HEAD_DIM, kv_width, 1)
    own_values = lax.dynamic_slice_in_dim(value_states, kv_first * HEAD_DIM, kv_width, 1)
    shift_count = (WINDOW + tok_rows - 2) // tok_rows
    block_bytes = 2 * residual.shape[0] * residual.shape[1]
    in_kernels = (
        col_count == 2 and row_count % 4 == 0 and row_count >= 8 and tok_rows % 64 == 0
        and kv_width % 128 == 0 and kv_width * col_count == key_states.shape[1]
        and 4 * row_count * block_bytes < VMEM_BYTES
    )
    routing = jnp.concatenate([expert_ids.astype(jnp.float32), route_weight], 1).T
    key_parts = []
    value_parts = []
    segment_parts = []
    start_parts = []
    if in_kernels:
        keys_before, values_before, segments_before = halo(
            key_states, value_states, segment_ids, row_count, shift_count, kv_width
        )
    for offset in range(shift_count, 0, -1):
        if in_kernels:
            arrived = (
                keys_before[offset - 1],
                values_before[offset - 1],
                segments_before[offset - 1, 0],
            )
        else:
            arrived = shifted((own_keys, own_values, segment_ids), "row", offset)
        key_parts.append(arrived[0])
        value_parts.append(arrived[1])
        segment_parts.append(arrived[2])
        start_parts.append((row_index - offset) * tok_rows)
    key_parts.append(own_keys)
    value_parts.append(own_values)
    segment_parts.append(segment_ids)
    start_parts.append(row_index * tok_rows)
    key_groups = jnp.concatenate(key_parts, 0).reshape(-1, kv_count, HEAD_DIM)
    value_groups = jnp.concatenate(value_parts, 0).reshape(-1, kv_count, HEAD_DIM)
    key_segments = jnp.concatenate(segment_parts, 0)
    positions = jnp.arange(tok_rows, dtype=jnp.int32)
    key_position = jnp.concatenate([start + positions for start in start_parts], 0)
    query_position = row_index * tok_rows + positions
    allowed = (key_position[None, :] >= 0) & (key_position[None, :] <= query_position[:, None])
    allowed = allowed & (key_position[None, :] > query_position[:, None] - WINDOW)
    allowed = allowed & (key_segments[None, :] == segment_ids[:, None])
    query_groups = query_states.reshape(tok_rows, kv_count, local_heads // kv_count, HEAD_DIM)
    sink_groups = sink_logits.reshape(kv_count, local_heads // kv_count, 1, 1)
    attended = attend(query_groups, key_groups, value_groups, allowed, sink_groups).reshape(
        tok_rows, local_heads * HEAD_DIM
    )
    partial_value = jnp.dot(attended, w_out, preferred_element_type=jnp.float32)
    feature_count = residual.shape[1] // col_count
    experts_all = w_gate_up.shape[0] * row_count
    slot_cap = max(2, 2 * TOP * tok_rows // experts_all)
    expert_gate_up = w_gate_up[0]
    expert_down = w_down[0]
    partial_value = partial_value.astype(jnp.bfloat16)
    if in_kernels:
        stream, gathered, routing = spread(partial_value, residual, norm_gain, routing, row_count)
    else:
        summed = lax.psum(partial_value, "col").astype(jnp.float32)
        stream = (residual.astype(jnp.float32) + summed).astype(jnp.bfloat16)
        gathered = lax.all_gather(normalize(stream, norm_gain), "row", axis=0, tiled=False)
        routing = lax.all_gather(routing, "row", axis=0, tiled=False)
    stream_part = lax.dynamic_slice_in_dim(stream, col_index * feature_count, feature_count, 1)
    names_mine = routing[:, :TOP] == row_index.astype(jnp.float32)
    mine = jnp.any(names_mine, axis=1)
    weight = jnp.sum(jnp.where(names_mine, routing[:, TOP:], 0.0), axis=1)
    slot_of = jnp.cumsum(mine.astype(jnp.int32), axis=1) - 1
    slots = jnp.arange(slot_cap, dtype=jnp.int32)
    chosen = mine[:, None, :] & (slot_of[:, None, :] == slots[None, :, None])
    selector = chosen.astype(jnp.bfloat16)
    combine = jnp.where(chosen, weight[:, None, :], 0.0)
    packed = jnp.einsum(
        "nst,ntd->nsd", selector, gathered, preferred_element_type=jnp.float32
    ).astype(jnp.bfloat16).reshape(row_count * slot_cap, -1)
    gate = jnp.dot(packed, expert_gate_up[0], preferred_element_type=jnp.float32)
    up = jnp.dot(packed, expert_gate_up[1], preferred_element_type=jnp.float32)
    active = ((up + 1.0) * gate * jax.nn.sigmoid(1.702 * gate)).astype(jnp.bfloat16)
    expert_partial = jnp.dot(active, expert_down, preferred_element_type=jnp.float32)
    scaled = expert_partial.reshape(row_count, slot_cap, -1) * jnp.sum(combine, 2)[:, :, None]
    mixed = jnp.einsum(
        "nst,nsd->ntd", selector, scaled.astype(jnp.bfloat16), preferred_element_type=jnp.float32
    ).astype(jnp.bfloat16)
    if in_kernels:
        mixed = fold(mixed, row_count, feature_count)
    else:
        mixed = mixed.reshape(row_count * tok_rows, -1)
        mixed = lax.psum_scatter(mixed, "row", scatter_dimension=0, tiled=True)
        mixed = lax.psum_scatter(mixed, "col", scatter_dimension=1, tiled=True)
    return (stream_part.astype(jnp.float32) + mixed.astype(jnp.float32)).astype(jnp.bfloat16)


def solution(mesh):
    in_specs = (
        P("row", None),
        P("row", "col"),
        P("row", None),
        P("row", None),
        P("row"),
        P("col"),
        P("col", None),
        P(),
        P("row", None),
        P("row", None),
        P("row", None, None, "col"),
        P("row", "col", None),
    )
    out_specs = P("row", "col")
    return jax.shard_map(local, mesh=mesh, in_specs=in_specs, out_specs=out_specs, check_vma=False)
```
